32 devices in a mesh: lon: 8 (over y, x, core), mem: 4 (over z).
Axes of the slice: x: 2, y: 2, z: 4, core: 2. Of those that a mesh axis runs over, the one named last changes fastest.
Arguments:
- sample_collection: bfloat16 [256, 3, 1, 16, 1024], P('mem', None, None, None, 'lon'), may hold values from -6 to 6
- layer_depth: float32 [1, 16, 1024], P(None, None, 'lon'), may hold values from 0.05 to 0.2
- obs_where: int32 [4, 8, 512], P('mem', 'lon'), may hold values from 0 to 4895, as said below
- observed_values: float32 [4, 8, 512], P('mem', 'lon'), may hold values from -6 to 6
- obs_precision: float32 [4, 8, 512], P('mem', 'lon'), may hold values from 0.5 to 4
- loc_index: int32 [4, 8, 512], P('mem', 'lon'), may hold values from 0 to 15
- obs_count: int32 [4, 8], P('mem', 'lon'), may hold values from 64 to 512, as said below
Outputs:
- analysis: bfloat16 [256, 3, 1, 16, 1024], P('mem', None, None, None, 'lon')
The draws below stay inside these ranges and needn't reach their ends.
Inputs may be any that keep to these rules, and one draw needn't show every extreme that they name: `obs_where`: flat index into a block's region of 3 x 1 x (12) x (136) cells (component, layer, row, column). Slots o < obs_count of a block hold observations; in each draw some block has all 512.
All inputs are finite; a program needn't handle non-finite values.
Results may differ from the reference program's by a relative error of at most 0.0037.
The reference program's roundings to bfloat16 on the way count: a program that leaves them out, or rounds other values in their place, can miss the bound.
Values may be sent and summed in bfloat16 or wider, within the bound.
A program may use at most 128 MiB of HBM per device.

```python
import math
import jax
import jax.numpy as jnp
from jax import lax

MEMBERS = 256
LEV = 1
STEPS = 2
MARGIN_WIDTH = 4
BAND = 4
CLON = 128
NOBS = 512
NS_ITERS = 5
BANDS = 4
STRIPS = 8
LAT = 16
NLON = 1024
N_LON = 8
N_MEM = 4


def draw_obs_where(key, part):
    row_span = BAND + 2 * MARGIN_WIDTH
    column_span = CLON + 2 * MARGIN_WIDTH
    key_field, key_row, key_column = jax.random.split(key, 3)
    layout = (N_MEM, N_LON, NOBS)
    field_pick = jax.random.randint(key_field, layout, 0, 3 * LEV)
    row_pick = jax.random.randint(key_row, layout, 0, row_span)
    column_pick = jax.random.randint(key_column, layout, 0, column_span)
    return ((field_pick * row_span + row_pick) * column_span + column_pick).astype(jnp.int32)


def draw_obs_count(key, part):
    key_base, key_star = jax.random.split(key, 2)
    base_count = jax.random.randint(key_base, (N_MEM, N_LON), NOBS // 8, NOBS + 1)
    chosen = jax.random.randint(key_star, (), 0, N_MEM * N_LON)
    position = jnp.arange(N_MEM * N_LON, dtype=jnp.int32).reshape(N_MEM, N_LON)
    return jnp.where(position == chosen, NOBS, base_count).astype(jnp.int32)


def plant(array, own_key, least, top_value):
    spot = [jax.random.randint(jax.random.fold_in(own_key, axis), (), 0, length) for axis, length in enumerate(array.shape)]
    widest = array.shape.index(max(array.shape))
    neighbour = spot[:widest] + [(spot[widest] + 1) % array.shape[widest]] + spot[widest + 1:]
    return array.at[tuple(spot)].set(least).at[tuple(neighbour)].set(top_value)


def block_levels(rng, extent, cuts, smallest, largest):
    def one(axis_at, blocks):
        heights = jax.random.uniform(jax.random.fold_in(jax.random.fold_in(rng, 6), axis_at), (blocks,), jnp.float32, smallest / len(cuts), largest / len(cuts))
        return jnp.repeat(jnp.exp(heights), extent[axis_at] // blocks).reshape((-1,) + (1,) * (len(extent) - axis_at - 1))

    gain = one(*cuts[0])
    for cut in cuts[1:]:
        gain = gain * one(*cut)
    return gain


def normal_values(rng, shape, deviation, most, cuts=(), kind=jnp.bfloat16):
    drawn = jax.random.normal(rng, shape, jnp.float32) * deviation
    if len(cuts) > 0:
        drawn = block_levels(rng, shape, cuts, -0.22, 0.18) * drawn
    return jnp.clip(drawn, min=-most, max=most).astype(kind)


def setup_inputs(seed: int = 0) -> dict:
    key_list = jax.random.split(jax.random.key(seed), 8)
    return {
        "sample_collection": normal_values(key_list[0], (MEMBERS, 3, LEV, LAT, NLON), 1.0, 6.0, ((0, 4), (4, 8))),
        "layer_depth": jnp.clip(0.05 + 0.15 * jax.random.uniform(key_list[1], (LEV, LAT, NLON), jnp.float32) ** block_levels(key_list[1], (LEV, LAT, NLON), ((2, 8),), -0.2, 0.2), 0.05, 0.2),
        "obs_where": draw_obs_where(jax.random.fold_in(key_list[7], 71), 0),
        "observed_values": normal_values(key_list[3], (BANDS, STRIPS, NOBS), 1.0, 6.0, ((0, 4), (1, 8)), jnp.float32),
        "obs_precision": jnp.clip(jnp.exp(math.log(4.0) - 2.0794415 * jax.random.uniform(key_list[4], (BANDS, STRIPS, NOBS), jnp.float32) ** block_levels(key_list[4], (BANDS, STRIPS, NOBS), ((0, 4), (1, 8)), -0.2, 0.2)), 0.5, 4.0),
        "loc_index": plant(jax.random.randint(key_list[5], (BANDS, STRIPS, NOBS), 0, 16), jax.random.fold_in(key_list[5], 1), 0, 15).astype(jnp.int32),
        "obs_count": draw_obs_count(jax.random.fold_in(key_list[7], 71), 0),
    }


time_step = 0.8
inflation = 1.1

def coriolis_rate(count_rows):
    latitude = jnp.arange(count_rows, dtype=jnp.float32)
    return 0.4 * (latitude / (count_rows - 1) - 0.5)

def lat_diff(field):
    bordered_array = jnp.pad(field, [(0, 0)] * (field.ndim - 2) + [(1, 1), (0, 0)])
    return 0.5 * (bordered_array[..., 2:, :] - bordered_array[..., :-2, :])

def lon_diff(field):
    return 0.5 * (field[..., 2:] - field[..., :-2])

def advance(fields, depth_cut, spin_frequency):
    height = fields[..., 0, :, :, :]
    east_wind = fields[..., 1, :, :, :]
    north_wind = fields[..., 2, :, :, :]
    flux_east = depth_cut * east_wind
    flux_north = depth_cut * north_wind
    height_new = height[..., 1:-1] - time_step * (lon_diff(flux_east) + lat_diff(flux_north)[..., 1:-1])
    east_new = east_wind[..., 2:-2] - time_step * lon_diff(height_new) + time_step * spin_frequency * north_wind[..., 2:-2]
    north_new = north_wind[..., 2:-2] - time_step * lat_diff(height_new)[..., 1:-1] - time_step * spin_frequency * east_wind[..., 2:-2]
    return jnp.stack([height_new[..., 1:-1], east_new, north_new], axis=-4)

def sample_prediction(sample_number, bordered_thickness_grid, spin_frequency):
    reach = 2 * STEPS
    enlarged_grid = jnp.pad(sample_number.astype(jnp.float32), ((0, 0), (0, 0), (0, 0), (reach, reach)), mode='wrap')
    total = bordered_thickness_grid.shape[-1]
    for step_index in range(STEPS):
        enlarged_grid = advance(enlarged_grid, bordered_thickness_grid[..., 2 * step_index:total - 2 * step_index], spin_frequency)
    return enlarged_grid.astype(jnp.bfloat16)

def analyse(region, where, values, precision_vals, locs, count):
    members = region.shape[0]
    highest = lax.Precision.HIGHEST
    flattened = region.reshape(members, -1)
    picked = jnp.take(flattened, where, axis=1).astype(jnp.float32)
    slot_index = jnp.arange(where.shape[0], dtype=jnp.int32)
    live_slots = (slot_index < count).astype(jnp.float32)
    taper_table = (1.0 - jnp.arange(16, dtype=jnp.float32) / 16.0) ** 2
    taper_weight = lax.optimization_barrier(jnp.sum(jnp.where(locs[:, None] == jnp.arange(16, dtype=jnp.int32)[None, :], taper_table[None, :], 0.0), axis=1))
    weight = precision_vals * taper_weight * live_slots
    obs_mean = lax.optimization_barrier(jnp.mean(picked, axis=0))
    spread = picked - obs_mean[None, :]
    innovation = values - obs_mean
    weighted = spread * weight[None, :]
    gram_matrix = jnp.dot(weighted, spread.T, precision=highest)
    drive_vector = jnp.dot(weighted, innovation, precision=highest)
    prior = (members - 1) / inflation
    trace_bound = prior + jnp.trace(gram_matrix)
    identity = jnp.eye(members, dtype=jnp.float32)
    root_iter = (gram_matrix + prior * identity) / trace_bound
    inv_root = identity
    for sweep in range(NS_ITERS):
        correction = 1.5 * identity - 0.5 * jnp.dot(inv_root, root_iter, precision=highest)
        root_iter = jnp.dot(root_iter, correction, precision=highest)
        inv_root = jnp.dot(correction, inv_root, precision=highest)
    shrink = inv_root / jnp.sqrt(trace_bound)
    mean_weight = jnp.dot(shrink, jnp.dot(shrink, drive_vector, precision=highest), precision=highest)
    weights = math.sqrt(members - 1) * shrink + mean_weight[:, None]
    owned_cells = region[:, :, :, MARGIN_WIDTH:MARGIN_WIDTH + BAND, MARGIN_WIDTH:MARGIN_WIDTH + CLON].reshape(members, -1).astype(jnp.float32)
    cell_mean = lax.optimization_barrier(jnp.mean(owned_cells, axis=0))
    perturb = owned_cells - cell_mean[None, :]
    analysed = cell_mean[None, :] + jnp.dot(weights.T, perturb, precision=highest)
    return analysed.astype(jnp.bfloat16).reshape(members, 3, LEV, BAND, CLON)

def reference(sample_collection, layer_depth, obs_where, observed_values, obs_precision, loc_index, obs_count):
    spin_frequency = coriolis_rate(LAT)[:, None]
    reach = 2 * STEPS
    bordered_thickness_grid = jnp.pad(layer_depth, ((0, 0), (0, 0), (reach, reach)), mode='wrap')
    predicted_solution = lax.map(lambda sample_number: sample_prediction(sample_number, bordered_thickness_grid, spin_frequency), sample_collection)
    bordered_array = jnp.pad(predicted_solution, ((0, 0), (0, 0), (0, 0), (MARGIN_WIDTH, MARGIN_WIDTH), (0, 0)))
    bordered_array = jnp.pad(bordered_array, ((0, 0), (0, 0), (0, 0), (0, 0), (MARGIN_WIDTH, MARGIN_WIDTH)), mode='wrap')
    zero = jnp.zeros((), jnp.int32)

    def analyse_device(device_index):
        band_index = (device_index // N_LON).astype(jnp.int32)
        strip_index = (device_index % N_LON).astype(jnp.int32)
        region = lax.dynamic_slice(bordered_array, (zero, zero, zero, band_index * BAND, strip_index * CLON), (MEMBERS, 3, LEV, BAND + 2 * MARGIN_WIDTH, CLON + 2 * MARGIN_WIDTH))
        return analyse(region, obs_where[band_index, strip_index], observed_values[band_index, strip_index], obs_precision[band_index, strip_index], loc_index[band_index, strip_index], obs_count[band_index, strip_index])
    analysed_blocks = lax.map(analyse_device, jnp.arange(N_MEM * N_LON, dtype=jnp.int32))
    analysed_blocks = analysed_blocks.reshape(N_MEM, N_LON, MEMBERS, 3, LEV, BAND, CLON)
    analysed_blocks = jnp.transpose(analysed_blocks, (2, 3, 4, 0, 5, 1, 6))
    return analysed_blocks.reshape(MEMBERS, 3, LEV, LAT, NLON)
```

```python
import functools
import math

import jax
import jax.numpy as jnp
from jax import lax
from jax.experimental import pallas as pl
from jax.experimental.pallas import tpu as pltpu
from jax.sharding import PartitionSpec as P

STEPS = 2
MARGIN_WIDTH = 4
BAND = 4
NS_ITERS = 5
EDGE = 8
CHUNK = 16
MESH = pl.DeviceIdType.MESH
HIGHEST = lax.Precision.HIGHEST

time_step = 0.8
inflation = 1.1
half_step = 0.5 * time_step


def iota(shape, axis):
    return lax.broadcasted_iota(jnp.int32, shape, axis)


def xor(me, mask):
    out = me
    bit = 1
    while bit <= mask:
        if mask & bit:
            out = out + bit - 2 * bit * lax.rem(me // bit, 2)
        bit *= 2
    return out


def spin(row, count_rows):
    return 0.4 * (row / (count_rows - 1) - 0.5)


def forecast_rows(h, u, v, depth):
    rows = len(h)
    wide = h[0].shape[-1]
    for _ in range(STEPS):
        flux_east = [depth[r] * u[r] for r in range(rows)]
        flux_north = [depth[r] * v[r] for r in range(rows)]
        h_new = []
        for r in range(rows):
            change = pltpu.roll(flux_east[r], wide - 1, 1) - pltpu.roll(flux_east[r], 1, 1)
            if r + 1 < rows:
                change = change + flux_north[r + 1]
            if r > 0:
                change = change - flux_north[r - 1]
            h_new.append(h[r] - half_step * change)
        u_new, v_new = [], []
        for r in range(rows):
            turn = time_step * spin(r, rows)
            slope = pltpu.roll(h_new[r], wide - 1, 1) - pltpu.roll(h_new[r], 1, 1)
            u_new.append(u[r] - half_step * slope + turn * v[r])
            new = v[r] - turn * u[r]
            if r + 1 < rows:
                new = new - half_step * h_new[r + 1]
            if r > 0:
                new = new + half_step * h_new[r - 1]
            v_new.append(new)
        h, u, v = h_new, u_new, v_new
    return h, u, v


def forecast_edge(left, right, depth_left, depth_right, rows):
    lanes = rows * EDGE
    at = iota((1, lanes), 1)
    place = lax.rem(at, EDGE)
    row = at // EDGE
    turn = time_step * 0.4 * (row.astype(jnp.float32) / (rows - 1) - 0.5)

    def shift(x, by):
        return pltpu.roll(x, by % lanes, 1)

    def lon(x_left, x_right):
        d_left = jnp.where(place == EDGE - 1, shift(x_right, EDGE - 1), shift(x_left, -1)) - shift(x_left, 1)
        d_right = shift(x_right, -1) - jnp.where(place == 0, shift(x_left, 1 - EDGE), shift(x_right, 1))
        return d_left, d_right

    def lat(x):
        north = jnp.where(row == rows - 1, 0.0, shift(x, -EDGE))
        south = jnp.where(row == 0, 0.0, shift(x, EDGE))
        return north - south

    for _ in range(STEPS):
        (h_l, u_l, v_l), (h_r, u_r, v_r) = left, right
        d_l, d_r = lon(depth_left * u_l, depth_right * u_r)
        n_l = h_l - half_step * (d_l + lat(depth_left * v_l))
        n_r = h_r - half_step * (d_r + lat(depth_right * v_r))
        s_l, s_r = lon(n_l, n_r)
        left = (n_l, u_l - half_step * s_l + turn * v_l, v_l - half_step * lat(n_l) - turn * u_l)
        right = (n_r, u_r - half_step * s_r + turn * v_r, v_r - half_step * lat(n_r) - turn * u_r)
    return left, right


def pack_depth(depth, side, strip):
    rows = depth.shape[0]
    lanes = rows * EDGE
    at = iota((1, lanes), 1)
    source = lax.rem(at, EDGE) + side * (strip - EDGE)
    spread = jnp.where(iota((strip, lanes), 0) == source, 1.0, 0.0)
    copies = jnp.dot(depth, spread, precision=HIGHEST, preferred_element_type=jnp.float32)
    kept = jnp.where(iota((rows, lanes), 0) == at // EDGE, copies, 0.0)
    return jnp.sum(kept, axis=0, keepdims=True)


def kernel(
    n, lons,
    x_ref, depth_ref, where_ref, values_ref, precision_ref, loc_ref, count_ref, out_ref,
    tall32, flat16, main32, edge_lo, edge_hi, west_hi, east_lo, depth_west, depth_east,
    wheres, fore, halo, cells, picks, picked, transform, result, back, out32,
    side_send, side_recv, where_send, where_recv, cell_send, cell_recv,
    pick_send, pick_recv, back_send, back_recv,
):
    me = lax.axis_index("mem")
    here = lax.axis_index("lon")
    east = lax.rem(here + 1, lons)
    west = lax.rem(here + lons - 1, lons)
    group, _, _, rows, strip = x_ref.shape
    members = n * group
    slots = where_ref.shape[-1]
    wide = strip + 2 * MARGIN_WIDTH
    band_rows = BAND + 2 * MARGIN_WIDTH
    area = band_rows * wide
    cell = BAND * strip
    lanes = rows * EDGE
    stack = 3 * rows
    masks = list(range(n - 1, 0, -1))
    peers = {mask: xor(me, mask) for mask in masks}

    barrier = pltpu.get_barrier_semaphore()
    for mask in masks:
        pl.semaphore_signal(barrier, inc=1, device_id={"mem": peers[mask]}, device_id_type=MESH)
    pl.semaphore_signal(barrier, inc=1, device_id={"lon": east}, device_id_type=MESH)
    pl.semaphore_signal(barrier, inc=1, device_id={"lon": west}, device_id_type=MESH)

    tall32[...] = x_ref[...].reshape(group * stack, strip).astype(jnp.float32)
    for c in range(3):
        for r in range(rows):
            row = tall32[pl.ds(c * rows + r, group, stride=stack), :]
            flat16[pl.ds(c * group, group), pl.ds(r * strip, strip)] = row.astype(jnp.bfloat16)

    per = min(rows, 128 // EDGE)
    at = iota((1, 2 * per * EDGE), 1)
    inner = lax.rem(at, per * EDGE)
    source = (inner // EDGE) * strip + lax.rem(inner, EDGE) + (at // (per * EDGE)) * (strip - EDGE)
    choose = jnp.where(iota((per * strip, 2 * per * EDGE), 0) == source, 1.0, 0.0).astype(jnp.bfloat16)
    for t in range(rows // per):
        part = jnp.dot(
            flat16[:, pl.ds(t * per * strip, per * strip)], choose, preferred_element_type=jnp.float32
        ).astype(jnp.bfloat16)
        edge_lo[:, pl.ds(t * per * EDGE, per * EDGE)] = part[:, : per * EDGE]
        edge_hi[:, pl.ds(t * per * EDGE, per * EDGE)] = part[:, per * EDGE :]

    pl.semaphore_wait(barrier, n + 1)

    def to_lon(src, dst, i, peer):
        return pltpu.make_async_remote_copy(
            src_ref=src, dst_ref=dst, send_sem=side_send.at[i], recv_sem=side_recv.at[i],
            device_id={"lon": peer}, device_id_type=MESH,
        )

    def to_mem(src, dst, ss, rs, mask):
        return pltpu.make_async_remote_copy(
            src_ref=src, dst_ref=dst, send_sem=ss, recv_sem=rs,
            device_id={"mem": peers[mask]}, device_id_type=MESH,
        )

    side_copies = [
        to_lon(edge_hi, west_hi, 0, east),
        to_lon(edge_lo, east_lo, 1, west),
        to_lon(depth_ref, depth_west, 2, east),
        to_lon(depth_ref, depth_east, 3, west),
    ]
    where_copies = [
        to_mem(where_ref, wheres.at[me], where_send.at[mask], where_recv.at[mask], mask) for mask in masks
    ]
    for copy in side_copies + where_copies:
        copy.start()
    wheres[me] = where_ref[...]

    @pl.loop(0, group // CHUNK)
    def _(i):
        base = i * (CHUNK * stack)
        state = [
            [tall32[pl.ds(base + c * rows + r, CHUNK, stride=stack), :] for r in range(rows)] for c in range(3)
        ]
        depth = [depth_ref[pl.ds(r, 1), :] for r in range(rows)]
        some = pl.ds(pl.multiple_of(i * CHUNK, CHUNK), CHUNK)
        for c, field in enumerate(forecast_rows(*state, depth)):
            for r in range(rows):
                main32[c * rows + r, some, :] = field[r]

    own_lo = pack_depth(depth_ref[...], 0, strip)
    own_hi = pack_depth(depth_ref[...], 1, strip)
    for copy in side_copies:
        copy.wait_recv()
    far_hi = pack_depth(depth_west[...], 1, strip)
    far_lo = pack_depth(depth_east[...], 0, strip)

    @pl.loop(0, group // CHUNK)
    def _(i):
        begin = pl.multiple_of(i * CHUNK, CHUNK)
        some = pl.ds(begin, CHUNK)

        def edge(ref):
            return [
                ref[pl.ds(pl.multiple_of(c * group + begin, CHUNK), CHUNK), :].astype(jnp.float32) for c in range(3)
            ]

        w_left, w_right = forecast_edge(edge(west_hi), edge(edge_lo), far_hi, own_lo, rows)
        e_left, e_right = forecast_edge(edge(edge_hi), edge(east_lo), own_hi, far_lo, rows)
        place = lax.rem(iota((1, lanes), 1), EDGE)
        column = iota((1, strip), 1)
        for c in range(3):
            outer = jnp.where(place >= MARGIN_WIDTH, w_left[c], e_right[c])
            halo[pl.ds(pl.multiple_of(c * group + begin, CHUNK), CHUNK), :] = outer.astype(jnp.bfloat16)
            rim = jnp.where(place < MARGIN_WIDTH, w_right[c], e_left[c])
            for t in range(rows // per):
                tile = rim[:, t * per * EDGE : (t + 1) * per * EDGE]
                turned = [tile] + [pltpu.roll(tile, (per - q) * EDGE, 1) for q in range(1, per)]
                for q in range(per):
                    r = t * per + q
                    value = main32[c * rows + r, some, :]
                    value = jnp.where(column < MARGIN_WIDTH, turned[q], value)
                    value = jnp.where(column >= strip - MARGIN_WIDTH, turned[(q + 1) % per], value)
                    fore[r // BAND, c, some, pl.ds((r % BAND) * strip, strip)] = value.astype(jnp.bfloat16)

    cell_copies = [
        [
            to_mem(fore.at[peers[mask], c], cells.at[c, me], cell_send.at[c, mask], cell_recv.at[c, mask], mask)
            for mask in masks
        ]
        for c in range(3)
    ]
    for copy in cell_copies[0]:
        copy.start()

    for copy in where_copies:
        copy.wait_recv()
    pick_copies = []
    for mask in masks + [0]:
        band = peers[mask] if mask else me
        index = wheres[band]
        component = jnp.where(index >= area, 1, 0) + jnp.where(index >= 2 * area, 1, 0)
        rest = index - component * area
        row = jnp.zeros_like(rest)
        for q in range(1, band_rows):
            row = row + jnp.where(rest >= q * wide, 1, 0)
        column = rest - row * wide - MARGIN_WIDTH
        block = jnp.where(row >= BAND, 1, 0) + jnp.where(row >= 2 * BAND, 1, 0)
        inside = jnp.logical_and(column >= 0, column < strip)
        target = jnp.where(inside, (row - block * BAND) * strip + column, -1)
        place = jnp.where(column < 0, column + EDGE, column - strip)
        rim_target = jnp.where(inside, -1, (band * BAND - MARGIN_WIDTH + row) * EDGE + place)
        hot = jnp.where(iota((cell, slots), 0) == target, 1.0, 0.0).astype(jnp.bfloat16)
        rim_hot = jnp.where(iota((lanes, slots), 0) == rim_target, 1.0, 0.0).astype(jnp.bfloat16)
        parts = [(c, e) for c in range(3) for e in range(3)]
        table = jnp.concatenate([fore[lax.rem(band + e + n - 1, n), c] for c, e in parts], axis=0)
        found = jnp.dot(table, hot, preferred_element_type=jnp.float32)
        rim_found = jnp.dot(halo[...], rim_hot, preferred_element_type=jnp.float32)
        total = jnp.zeros((group, slots), jnp.float32)
        for q, (c, e) in enumerate(parts):
            exists = jnp.logical_and(band + e - 1 >= 0, band + e - 1 < n)
            wanted = jnp.where(exists, 3 * c + e, -1)
            total = jnp.where(3 * component + block == wanted, found[q * group : (q + 1) * group], total)
        for c in range(3):
            rim_part = rim_found[c * group : (c + 1) * group]
            total = total + jnp.where(component == c, rim_part, 0.0)
        if mask:
            picks[mask] = total.astype(jnp.bfloat16)
            copy = to_mem(picks.at[mask], picked.at[me], pick_send.at[mask], pick_recv.at[mask], mask)
            copy.start()
            pick_copies.append(copy)
        else:
            picked[me] = total.astype(jnp.bfloat16)

    for c in range(1, 3):
        for copy in cell_copies[c]:
            copy.start()
    for c in range(3):
        cells[c, me] = fore[me, c]

    live = jnp.where(iota((1, slots), 1) < count_ref[...], 1.0, 0.0)
    taper = 1.0 - loc_ref[...].astype(jnp.float32) / 16.0
    weight = precision_ref[...] * (taper * taper) * live

    for copy in pick_copies:
        copy.wait_recv()
    obs = picked[...].astype(jnp.float32).reshape(members, slots)
    obs_mean = jnp.mean(obs, axis=0, keepdims=True)
    spread = obs - obs_mean
    weighted = spread * weight
    innovation = values_ref[...] - obs_mean

    def mm(a, b):
        return jnp.dot(a, b, precision=HIGHEST, preferred_element_type=jnp.float32)

    gram = lax.dot_general(
        weighted, spread, (((1,), (1,)), ((), ())),
        precision=HIGHEST, preferred_element_type=jnp.float32,
    )
    drive = jnp.sum(weighted * innovation, axis=1, keepdims=True)
    prior = (members - 1) / inflation
    trace = jnp.sum(jnp.sum(weighted * spread, axis=1, keepdims=True), axis=0, keepdims=True)
    trace_bound = prior + trace
    identity = jnp.where(iota((members, members), 0) == iota((members, members), 1), 1.0, 0.0)
    root_iter = (gram + prior * identity) / trace_bound
    correction = 1.5 * identity - 0.5 * root_iter
    root_iter = mm(root_iter, correction)
    inv_root = correction
    for sweep in range(1, NS_ITERS):
        correction = 1.5 * identity - 0.5 * mm(inv_root, root_iter)
        if sweep < NS_ITERS - 1:
            root_iter = mm(root_iter, correction)
        inv_root = mm(correction, inv_root)
    shrink = inv_root * lax.rsqrt(trace_bound)
    inner = jnp.sum(shrink * drive, axis=0, keepdims=True)
    mean_weight = jnp.sum(shrink * inner, axis=1, keepdims=True)
    weights = math.sqrt(members - 1) * shrink + mean_weight
    weights = weights + (1.0 - jnp.sum(weights, axis=0, keepdims=True)) / members
    weights_t = weights.T
    high = weights_t.astype(jnp.bfloat16)
    transform[0] = high
    transform[1] = (weights_t - high.astype(jnp.float32)).astype(jnp.bfloat16)

    back_copies = []
    for c in range(3):
        for copy in cell_copies[c]:
            copy.wait_recv()
        all_cells = cells[c].reshape(members, cell)
        total = jnp.dot(transform[0], all_cells, preferred_element_type=jnp.float32)
        total += jnp.dot(transform[1], all_cells, preferred_element_type=jnp.float32)
        result[c] = total.astype(jnp.bfloat16).reshape(n, group, cell)
        row_copies = [
            to_mem(result.at[c, peers[mask]], back.at[c, me], back_send.at[c, mask], back_recv.at[c, mask], mask)
            for mask in masks
        ]
        for copy in row_copies:
            copy.start()
        back_copies.append(row_copies)
        back[c, me] = result[c, me]

    def place_rows(c, band):
        block = back[c, band].astype(jnp.float32)
        for q in range(BAND):
            out32[c, pl.ds(band * BAND + q, group, stride=rows), :] = block[:, q * strip : (q + 1) * strip]

    for c in range(3):
        place_rows(c, me)
        for copy, mask in zip(back_copies[c], masks):
            copy.wait_recv()
            place_rows(c, peers[mask])
        out_ref[:, c, 0] = out32[c].reshape(group, rows, strip).astype(jnp.bfloat16)

    for copy in side_copies + where_copies + pick_copies:
        copy.wait_send()
    for c in range(3):
        for copy in cell_copies[c] + back_copies[c]:
            copy.wait_send()


def on_device(
    sample_collection, layer_depth, obs_where, observed_values, obs_precision, loc_index, obs_count
):
    n, lons = lax.axis_size("mem"), lax.axis_size("lon")
    group, _, _, rows, strip = sample_collection.shape
    slots = obs_where.shape[-1]
    members, lanes, cell = n * group, rows * EDGE, BAND * strip
    vmem = pl.BlockSpec(memory_space=pltpu.VMEM)
    dma = pltpu.SemaphoreType.DMA
    f32, bf16 = jnp.float32, jnp.bfloat16
    scratch = [
        pltpu.VMEM((group * 3 * rows, strip), f32),
        pltpu.VMEM((3 * group, rows * strip), bf16),
        pltpu.VMEM((3 * rows, group, strip), f32),
    ]
    scratch += [pltpu.VMEM((3 * group, lanes), bf16)] * 4
    scratch += [pltpu.VMEM((rows, strip), f32)] * 2
    scratch += [
        pltpu.VMEM((n, 1, slots), jnp.int32),
        pltpu.VMEM((n, 3, group, cell), bf16),
        pltpu.VMEM((3 * group, lanes), bf16),
        pltpu.VMEM((3, n, group, cell), bf16),
        pltpu.VMEM((n, group, slots), bf16),
        pltpu.VMEM((n, group, slots), bf16),
        pltpu.VMEM((2, members, members), bf16),
        pltpu.VMEM((3, n, group, cell), bf16),
        pltpu.VMEM((3, n, group, cell), bf16),
        pltpu.VMEM((3, group * rows, strip), f32),
    ]
    scratch += [dma((4,))] * 2 + [dma((n,))] * 2 + [dma((3, n))] * 2 + [dma((n,))] * 2 + [dma((3, n))] * 2
    return pl.pallas_call(
        functools.partial(kernel, n, lons),
        out_shape=jax.ShapeDtypeStruct(sample_collection.shape, bf16),
        in_specs=[vmem] * 7,
        out_specs=vmem,
        scratch_shapes=scratch,
        compiler_params=pltpu.CompilerParams(
            collective_id=0, has_side_effects=True, vmem_limit_bytes=60 * 1024 * 1024
        ),
    )(
        sample_collection, layer_depth[0], obs_where[0], observed_values[0],
        obs_precision[0], loc_index[0], obs_count,
    )


def solution(mesh):
    in_specs = (
        P("mem", None, None, None, "lon"),
        P(None, None, "lon"),
        P("mem", "lon", None),
        P("mem", "lon", None),
        P("mem", "lon", None),
        P("mem", "lon", None),
        P("mem", "lon"),
    )
    out_specs = P("mem", None, None, None, "lon")
    return jax.shard_map(
        on_device, mesh=mesh, in_specs=in_specs, out_specs=out_specs, check_vma=False
    )
```

```python
import functools
import math

import jax
import jax.numpy as jnp
from jax import lax
from jax.experimental import pallas as pl
from jax.experimental.pallas import tpu as pltpu
from jax.sharding import PartitionSpec as P

STEPS = 2
MARGIN_WIDTH = 4
BAND = 4
NS_ITERS = 5
EDGE = 8
CHUNK = 16
MESH = pl.DeviceIdType.MESH
HIGHEST = lax.Precision.HIGHEST

time_step = 0.8
inflation = 1.1
half_step = 0.5 * time_step


def iota(shape, axis):
    return lax.broadcasted_iota(jnp.int32, shape, axis)


def xor(me, mask):
    out = me
    bit = 1
    while bit <= mask:
        if mask & bit:
            out = out + bit - 2 * bit * lax.rem(me // bit, 2)
        bit *= 2
    return out


def spin(row, count_rows):
    return 0.4 * (row / (count_rows - 1) - 0.5)


def forecast_rows(h, u, v, depth):
    rows = len(h)
    wide = h[0].shape[-1]
    for _ in range(STEPS):
        flux_east = [depth[r] * u[r] for r in range(rows)]
        flux_north = [depth[r] * v[r] for r in range(rows)]
        h_new = []
        for r in range(rows):
            change = pltpu.roll(flux_east[r], wide - 1, 1) - pltpu.roll(flux_east[r], 1, 1)
            if r + 1 < rows:
                change = change + flux_north[r + 1]
            if r > 0:
                change = change - flux_north[r - 1]
            h_new.append(h[r] - half_step * change)
        u_new, v_new = [], []
        for r in range(rows):
            turn = time_step * spin(r, rows)
            slope = pltpu.roll(h_new[r], wide - 1, 1) - pltpu.roll(h_new[r], 1, 1)
            u_new.append(u[r] - half_step * slope + turn * v[r])
            new = v[r] - turn * u[r]
            if r + 1 < rows:
                new = new - half_step * h_new[r + 1]
            if r > 0:
                new = new + half_step * h_new[r - 1]
            v_new.append(new)
        h, u, v = h_new, u_new, v_new
    return h, u, v


def forecast_edge(left, right, depth_left, depth_right, rows):
    lanes = rows * EDGE
    at = iota((1, lanes), 1)
    place = lax.rem(at, EDGE)
    row = at // EDGE
    turn = time_step * 0.4 * (row.astype(jnp.float32) / (rows - 1) - 0.5)

    def shift(x, by):
        return pltpu.roll(x, by % lanes, 1)

    def lon(x_left, x_right):
        d_left = jnp.where(place == EDGE - 1, shift(x_right, EDGE - 1), shift(x_left, -1)) - shift(x_left, 1)
        d_right = shift(x_right, -1) - jnp.where(place == 0, shift(x_left, 1 - EDGE), shift(x_right, 1))
        return d_left, d_right

    def lat(x):
        north = jnp.where(row == rows - 1, 0.0, shift(x, -EDGE))
        south = jnp.where(row == 0, 0.0, shift(x, EDGE))
        return north - south

    for _ in range(STEPS):
        (h_l, u_l, v_l), (h_r, u_r, v_r) = left, right
        d_l, d_r = lon(depth_left * u_l, depth_right * u_r)
        n_l = h_l - half_step * (d_l + lat(depth_left * v_l))
        n_r = h_r - half_step * (d_r + lat(depth_right * v_r))
        s_l, s_r = lon(n_l, n_r)
        left = (n_l, u_l - half_step * s_l + turn * v_l, v_l - half_step * lat(n_l) - turn * u_l)
        right = (n_r, u_r - half_step * s_r + turn * v_r, v_r - half_step * lat(n_r) - turn * u_r)
    return left, right


def pack_depth(depth, side, strip):
    rows = depth.shape[0]
    lanes = rows * EDGE
    at = iota((1, lanes), 1)
    source = lax.rem(at, EDGE) + side * (strip - EDGE)
    spread = jnp.where(iota((strip, lanes), 0) == source, 1.0, 0.0)
    copies = jnp.dot(depth, spread, precision=HIGHEST, preferred_element_type=jnp.float32)
    kept = jnp.where(iota((rows, lanes), 0) == at // EDGE, copies, 0.0)
    return jnp.sum(kept, axis=0, keepdims=True)


def kernel(
    n, lons,
    x_hbm, depth_hbm, where_hbm, values_hbm, precision_hbm, loc_hbm, count_hbm, out_ref,
    x_ref, depth_ref, values_ref, precision_ref, loc_ref, count_ref, tall32, flat16, main32, edge_lo, edge_hi, west_hi, east_lo, depth_west, depth_east,
    wheres, fore, halo, cells, picks, picked, transform, result, back, out32, local_sem,
    side_send, side_recv, where_send, where_recv, cell_send, cell_recv,
    pick_send, pick_recv, back_send, back_recv,
):
    me = lax.axis_index("mem")
    here = lax.axis_index("lon")
    east = lax.rem(here + 1, lons)
    west = lax.rem(here + lons - 1, lons)
    group, _, _, rows, strip = x_ref.shape
    members = n * group
    slots = where_hbm.shape[-1]
    wide = strip + 2 * MARGIN_WIDTH
    band_rows = BAND + 2 * MARGIN_WIDTH
    area = band_rows * wide
    cell = BAND * strip
    lanes = rows * EDGE
    stack = 3 * rows
    masks = list(range(n - 1, 0, -1))
    peers = {mask: xor(me, mask) for mask in masks}
    local_copies = [
        pltpu.make_async_copy(src, dst, local_sem.at[i])
        for i, (src, dst) in enumerate([
            (x_hbm, x_ref), (depth_hbm, depth_ref), (where_hbm, wheres.at[me]), (values_hbm, values_ref),
            (precision_hbm, precision_ref), (loc_hbm, loc_ref), (count_hbm, count_ref),
        ])
    ]

    barrier = pltpu.get_barrier_semaphore()
    for mask in masks:
        pl.semaphore_signal(barrier, inc=1, device_id={"mem": peers[mask]}, device_id_type=MESH)
    pl.semaphore_signal(barrier, inc=1, device_id={"lon": east}, device_id_type=MESH)
    pl.semaphore_signal(barrier, inc=1, device_id={"lon": west}, device_id_type=MESH)

    for copy in local_copies:
        copy.start()

    local_copies[0].wait()
    tall32[...] = x_ref[...].reshape(group * stack, strip).astype(jnp.float32)
    for c in range(3):
        for r in range(rows):
            row = tall32[pl.ds(c * rows + r, group, stride=stack), :]
            flat16[pl.ds(c * group, group), pl.ds(r * strip, strip)] = row.astype(jnp.bfloat16)

    per = min(rows, 128 // EDGE)
    at = iota((1, 2 * per * EDGE), 1)
    inner = lax.rem(at, per * EDGE)
    source = (inner // EDGE) * strip + lax.rem(inner, EDGE) + (at // (per * EDGE)) * (strip - EDGE)
    choose = jnp.where(iota((per * strip, 2 * per * EDGE), 0) == source, 1.0, 0.0).astype(jnp.bfloat16)
    for t in range(rows // per):
        part = jnp.dot(
            flat16[:, pl.ds(t * per * strip, per * strip)], choose, preferred_element_type=jnp.float32
        ).astype(jnp.bfloat16)
        edge_lo[:, pl.ds(t * per * EDGE, per * EDGE)] = part[:, : per * EDGE]
        edge_hi[:, pl.ds(t * per * EDGE, per * EDGE)] = part[:, per * EDGE :]

    pl.semaphore_wait(barrier, n + 1)

    def to_lon(src, dst, i, peer):
        return pltpu.make_async_remote_copy(
            src_ref=src, dst_ref=dst, send_sem=side_send.at[i], recv_sem=side_recv.at[i],
            device_id={"lon": peer}, device_id_type=MESH,
        )

    def to_mem(src, dst, ss, rs, mask):
        return pltpu.make_async_remote_copy(
            src_ref=src, dst_ref=dst, send_sem=ss, recv_sem=rs,
            device_id={"mem": peers[mask]}, device_id_type=MESH,
        )

    side_copies = [
        to_lon(edge_hi, west_hi, 0, east),
        to_lon(edge_lo, east_lo, 1, west),
        to_lon(depth_hbm, depth_west, 2, east),
        to_lon(depth_hbm, depth_east, 3, west),
    ]
    where_copies = [
        to_mem(where_hbm, wheres.at[me], where_send.at[mask], where_recv.at[mask], mask) for mask in masks
    ]
    for copy in side_copies + where_copies:
        copy.start()

    local_copies[1].wait()

    @pl.loop(0, group // CHUNK)
    def _(i):
        base = i * (CHUNK * stack)
        state = [
            [tall32[pl.ds(base + c * rows + r, CHUNK, stride=stack), :] for r in range(rows)] for c in range(3)
        ]
        depth = [depth_ref[pl.ds(r, 1), :] for r in range(rows)]
        some = pl.ds(pl.multiple_of(i * CHUNK, CHUNK), CHUNK)
        for c, field in enumerate(forecast_rows(*state, depth)):
            for r in range(rows):
                main32[c * rows + r, some, :] = field[r]

    own_lo = pack_depth(depth_ref[...], 0, strip)
    own_hi = pack_depth(depth_ref[...], 1, strip)
    for copy in side_copies:
        copy.wait_recv()
    far_hi = pack_depth(depth_west[...], 1, strip)
    far_lo = pack_depth(depth_east[...], 0, strip)

    @pl.loop(0, group // CHUNK)
    def _(i):
        begin = pl.multiple_of(i * CHUNK, CHUNK)
        some = pl.ds(begin, CHUNK)

        def edge(ref):
            return [
                ref[pl.ds(pl.multiple_of(c * group + begin, CHUNK), CHUNK), :].astype(jnp.float32) for c in range(3)
            ]

        w_left, w_right = forecast_edge(edge(west_hi), edge(edge_lo), far_hi, own_lo, rows)
        e_left, e_right = forecast_edge(edge(edge_hi), edge(east_lo), own_hi, far_lo, rows)
        place = lax.rem(iota((1, lanes), 1), EDGE)
        column = iota((1, strip), 1)
        for c in range(3):
            outer = jnp.where(place >= MARGIN_WIDTH, w_left[c], e_right[c])
            halo[pl.ds(pl.multiple_of(c * group + begin, CHUNK), CHUNK), :] = outer.astype(jnp.bfloat16)
            rim = jnp.where(place < MARGIN_WIDTH, w_right[c], e_left[c])
            for t in range(rows // per):
                tile = rim[:, t * per * EDGE : (t + 1) * per * EDGE]
                turned = [tile] + [pltpu.roll(tile, (per - q) * EDGE, 1) for q in range(1, per)]
                for q in range(per):
                    r = t * per + q
                    value = main32[c * rows + r, some, :]
                    value = jnp.where(column < MARGIN_WIDTH, turned[q], value)
                    value = jnp.where(column >= strip - MARGIN_WIDTH, turned[(q + 1) % per], value)
                    fore[r // BAND, c, some, pl.ds((r % BAND) * strip, strip)] = value.astype(jnp.bfloat16)

    cell_copies = [
        [
            to_mem(fore.at[peers[mask], c], cells.at[c, me], cell_send.at[c, mask], cell_recv.at[c, mask], mask)
            for mask in masks
        ]
        for c in range(3)
    ]
    for copy in cell_copies[0]:
        copy.start()

    for copy in where_copies:
        copy.wait_recv()
    local_copies[2].wait()
    pick_copies = []
    for mask in masks + [0]:
        band = peers[mask] if mask else me
        index = wheres[band]
        component = jnp.where(index >= area, 1, 0) + jnp.where(index >= 2 * area, 1, 0)
        rest = index - component * area
        row = jnp.zeros_like(rest)
        for q in range(1, band_rows):
            row = row + jnp.where(rest >= q * wide, 1, 0)
        column = rest - row * wide - MARGIN_WIDTH
        block = jnp.where(row >= BAND, 1, 0) + jnp.where(row >= 2 * BAND, 1, 0)
        inside = jnp.logical_and(column >= 0, column < strip)
        target = jnp.where(inside, (row - block * BAND) * strip + column, -1)
        place = jnp.where(column < 0, column + EDGE, column - strip)
        rim_target = jnp.where(inside, -1, (band * BAND - MARGIN_WIDTH + row) * EDGE + place)
        hot = jnp.where(iota((cell, slots), 0) == target, 1.0, 0.0).astype(jnp.bfloat16)
        rim_hot = jnp.where(iota((lanes, slots), 0) == rim_target, 1.0, 0.0).astype(jnp.bfloat16)
        parts = [(c, e) for c in range(3) for e in range(3)]
        table = jnp.concatenate([fore[lax.rem(band + e + n - 1, n), c] for c, e in parts], axis=0)
        found = jnp.dot(table, hot, preferred_element_type=jnp.float32)
        rim_found = jnp.dot(halo[...], rim_hot, preferred_element_type=jnp.float32)
        total = jnp.zeros((group, slots), jnp.float32)
        for q, (c, e) in enumerate(parts):
            exists = jnp.logical_and(band + e - 1 >= 0, band + e - 1 < n)
            wanted = jnp.where(exists, 3 * c + e, -1)
            total = jnp.where(3 * component + block == wanted, found[q * group : (q + 1) * group], total)
        for c in range(3):
            rim_part = rim_found[c * group : (c + 1) * group]
            total = total + jnp.where(component == c, rim_part, 0.0)
        if mask:
            picks[mask] = total.astype(jnp.bfloat16)
            copy = to_mem(picks.at[mask], picked.at[me], pick_send.at[mask], pick_recv.at[mask], mask)
            copy.start()
            pick_copies.append(copy)
        else:
            picked[me] = total.astype(jnp.bfloat16)

    for c in range(1, 3):
        for copy in cell_copies[c]:
            copy.start()
    for c in range(3):
        cells[c, me] = fore[me, c]

    for copy in local_copies[3:]:
        copy.wait()
    live = jnp.where(iota((1, slots), 1) < count_ref[...], 1.0, 0.0)
    taper = 1.0 - loc_ref[...].astype(jnp.float32) / 16.0
    weight = precision_ref[...] * (taper * taper) * live

    for copy in pick_copies:
        copy.wait_recv()
    obs = picked[...].astype(jnp.float32).reshape(members, slots)
    obs_mean = jnp.mean(obs, axis=0, keepdims=True)
    spread = obs - obs_mean
    weighted = spread * weight
    innovation = values_ref[...] - obs_mean

    def mm(a, b):
        return jnp.dot(a, b, precision=HIGHEST, preferred_element_type=jnp.float32)

    gram = lax.dot_general(
        weighted, spread, (((1,), (1,)), ((), ())),
        precision=HIGHEST, preferred_element_type=jnp.float32,
    )
    drive = jnp.sum(weighted * innovation, axis=1, keepdims=True)
    prior = (members - 1) / inflation
    trace = jnp.sum(jnp.sum(weighted * spread, axis=1, keepdims=True), axis=0, keepdims=True)
    trace_bound = prior + trace
    identity = jnp.where(iota((members, members), 0) == iota((members, members), 1), 1.0, 0.0)
    root_iter = (gram + prior * identity) / trace_bound
    correction = 1.5 * identity - 0.5 * root_iter
    root_iter = mm(root_iter, correction)
    inv_root = correction
    for sweep in range(1, NS_ITERS):
        correction = 1.5 * identity - 0.5 * mm(inv_root, root_iter)
        if sweep < NS_ITERS - 1:
            root_iter = mm(root_iter, correction)
        inv_root = mm(correction, inv_root)
    shrink = inv_root * lax.rsqrt(trace_bound)
    inner = jnp.sum(shrink * drive, axis=0, keepdims=True)
    mean_weight = jnp.sum(shrink * inner, axis=1, keepdims=True)
    weights = math.sqrt(members - 1) * shrink + mean_weight
    weights = weights + (1.0 - jnp.sum(weights, axis=0, keepdims=True)) / members
    weights_t = weights.T
    high = weights_t.astype(jnp.bfloat16)
    transform[0] = high
    transform[1] = (weights_t - high.astype(jnp.float32)).astype(jnp.bfloat16)

    back_copies = []
    for c in range(3):
        for copy in cell_copies[c]:
            copy.wait_recv()
        all_cells = cells[c].reshape(members, cell)
        total = jnp.dot(transform[0], all_cells, preferred_element_type=jnp.float32)
        total += jnp.dot(transform[1], all_cells, preferred_element_type=jnp.float32)
        result[c] = total.astype(jnp.bfloat16).reshape(n, group, cell)
        row_copies = [
            to_mem(result.at[c, peers[mask]], back.at[c, me], back_send.at[c, mask], back_recv.at[c, mask], mask)
            for mask in masks
        ]
        for copy in row_copies:
            copy.start()
        back_copies.append(row_copies)
        back[c, me] = result[c, me]

    def place_rows(c, band):
        block = back[c, band].astype(jnp.float32)
        for q in range(BAND):
            out32[c, pl.ds(band * BAND + q, group, stride=rows), :] = block[:, q * strip : (q + 1) * strip]

    for c in range(3):
        place_rows(c, me)
        for copy, mask in zip(back_copies[c], masks):
            copy.wait_recv()
            place_rows(c, peers[mask])
        out_ref[:, c, 0] = out32[c].reshape(group, rows, strip).astype(jnp.bfloat16)

    for copy in side_copies + where_copies + pick_copies:
        copy.wait_send()
    for c in range(3):
        for copy in cell_copies[c] + back_copies[c]:
            copy.wait_send()


def deliver(in_ref, out_ref, sem):
    copy = pltpu.make_async_copy(in_ref, out_ref, sem)
    copy.start()
    copy.wait()


def on_device(
    sample_collection, layer_depth, obs_where, observed_values, obs_precision, loc_index, obs_count
):
    n, lons = lax.axis_size("mem"), lax.axis_size("lon")
    group, _, _, rows, strip = sample_collection.shape
    slots = obs_where.shape[-1]
    members, lanes, cell = n * group, rows * EDGE, BAND * strip
    vmem = pl.BlockSpec(memory_space=pltpu.VMEM)
    dma = pltpu.SemaphoreType.DMA
    f32, bf16 = jnp.float32, jnp.bfloat16
    scratch = [
        pltpu.VMEM(sample_collection.shape, bf16),
        pltpu.VMEM((rows, strip), f32),
        pltpu.VMEM((1, slots), f32),
        pltpu.VMEM((1, slots), f32),
        pltpu.VMEM((1, slots), jnp.int32),
        pltpu.VMEM((1, 1), jnp.int32),
        pltpu.VMEM((group * 3 * rows, strip), f32),
        pltpu.VMEM((3 * group, rows * strip), bf16),
        pltpu.VMEM((3 * rows, group, strip), f32),
    ]
    scratch += [pltpu.VMEM((3 * group, lanes), bf16)] * 4
    scratch += [pltpu.VMEM((rows, strip), f32)] * 2
    scratch += [
        pltpu.VMEM((n, 1, slots), jnp.int32),
        pltpu.VMEM((n, 3, group, cell), bf16),
        pltpu.VMEM((3 * group, lanes), bf16),
        pltpu.VMEM((3, n, group, cell), bf16),
        pltpu.VMEM((n, group, slots), bf16),
        pltpu.VMEM((n, group, slots), bf16),
        pltpu.VMEM((2, members, members), bf16),
        pltpu.VMEM((3, n, group, cell), bf16),
        pltpu.VMEM((3, n, group, cell), bf16),
        pltpu.VMEM((3, group * rows, strip), f32),
    ]
    scratch += [dma((7,))]
    scratch += [dma((4,))] * 2 + [dma((n,))] * 2 + [dma((3, n))] * 2 + [dma((n,))] * 2 + [dma((3, n))] * 2
    out = pl.pallas_call(
        functools.partial(kernel, n, lons),
        out_shape=pltpu.VMEM(sample_collection.shape, bf16),
        in_specs=[pl.BlockSpec(memory_space=pltpu.HBM)] * 7,
        out_specs=vmem,
        scratch_shapes=scratch,
        compiler_params=pltpu.CompilerParams(
            collective_id=0, has_side_effects=True, vmem_limit_bytes=60 * 1024 * 1024
        ),
    )(
        sample_collection, layer_depth[0], obs_where[0], observed_values[0],
        obs_precision[0], loc_index[0], obs_count,
    )
    return pl.pallas_call(
        deliver,
        out_shape=jax.ShapeDtypeStruct(sample_collection.shape, bf16),
        in_specs=[vmem],
        out_specs=pl.BlockSpec(memory_space=pl.ANY),
        scratch_shapes=[dma(())],
        compiler_params=pltpu.CompilerParams(vmem_limit_bytes=4 * 1024 * 1024),
    )(out)


def solution(mesh):
    in_specs = (
        P("mem", None, None, None, "lon"),
        P(None, None, "lon"),
        P("mem", "lon", None),
        P("mem", "lon", None),
        P("mem", "lon", None),
        P("mem", "lon", None),
        P("mem", "lon"),
    )
    out_specs = P("mem", None, None, None, "lon")
    return jax.shard_map(
        on_device, mesh=mesh, in_specs=in_specs, out_specs=out_specs, check_vma=False
    )
```

```python
import functools
import math

import jax
import jax.numpy as jnp
from jax import lax
from jax.experimental import pallas as pl
from jax.experimental.pallas import tpu as pltpu
from jax.sharding import PartitionSpec as P

STEPS = 2
MARGIN_WIDTH = 4
BAND = 4
NS_ITERS = 5
EDGE = 8
CHUNK = 16
MESH = pl.DeviceIdType.MESH
HIGHEST = lax.Precision.HIGHEST

time_step = 0.8
inflation = 1.1
half_step = 0.5 * time_step


def iota(shape, axis):
    return lax.broadcasted_iota(jnp.int32, shape, axis)


def xor(me, mask):
    out = me
    bit = 1
    while bit <= mask:
        if mask & bit:
            out = out + bit - 2 * bit * lax.rem(me // bit, 2)
        bit *= 2
    return out


def spin(row, count_rows):
    return 0.4 * (row / (count_rows - 1) - 0.5)


def forecast_rows(h, u, v, depth):
    rows = len(h)
    wide = h[0].shape[-1]
    for _ in range(STEPS):
        flux_east = [depth[r] * u[r] for r in range(rows)]
        flux_north = [depth[r] * v[r] for r in range(rows)]
        h_new = []
        for r in range(rows):
            change = pltpu.roll(flux_east[r], wide - 1, 1) - pltpu.roll(flux_east[r], 1, 1)
            if r + 1 < rows:
                change = change + flux_north[r + 1]
            if r > 0:
                change = change - flux_north[r - 1]
            h_new.append(h[r] - half_step * change)
        u_new, v_new = [], []
        for r in range(rows):
            turn = time_step * spin(r, rows)
            slope = pltpu.roll(h_new[r], wide - 1, 1) - pltpu.roll(h_new[r], 1, 1)
            u_new.append(u[r] - half_step * slope + turn * v[r])
            new = v[r] - turn * u[r]
            if r + 1 < rows:
                new = new - half_step * h_new[r + 1]
            if r > 0:
                new = new + half_step * h_new[r - 1]
            v_new.append(new)
        h, u, v = h_new, u_new, v_new
    return h, u, v


def forecast_edge(left, right, depth_left, depth_right, rows):
    lanes = rows * EDGE
    at = iota((1, lanes), 1)
    place = lax.rem(at, EDGE)
    row = at // EDGE
    turn = time_step * 0.4 * (row.astype(jnp.float32) / (rows - 1) - 0.5)

    def shift(x, by):
        return pltpu.roll(x, by % lanes, 1)

    def lon(x_left, x_right):
        d_left = jnp.where(place == EDGE - 1, shift(x_right, EDGE - 1), shift(x_left, -1)) - shift(x_left, 1)
        d_right = shift(x_right, -1) - jnp.where(place == 0, shift(x_left, 1 - EDGE), shift(x_right, 1))
        return d_left, d_right

    def lat(x):
        north = jnp.where(row == rows - 1, 0.0, shift(x, -EDGE))
        south = jnp.where(row == 0, 0.0, shift(x, EDGE))
        return north - south

    for _ in range(STEPS):
        (h_l, u_l, v_l), (h_r, u_r, v_r) = left, right
        d_l, d_r = lon(depth_left * u_l, depth_right * u_r)
        n_l = h_l - half_step * (d_l + lat(depth_left * v_l))
        n_r = h_r - half_step * (d_r + lat(depth_right * v_r))
        s_l, s_r = lon(n_l, n_r)
        left = (n_l, u_l - half_step * s_l + turn * v_l, v_l - half_step * lat(n_l) - turn * u_l)
        right = (n_r, u_r - half_step * s_r + turn * v_r, v_r - half_step * lat(n_r) - turn * u_r)
    return left, right


def pack_depth(depth, side, strip):
    rows = depth.shape[0]
    lanes = rows * EDGE
    at = iota((1, lanes), 1)
    source = lax.rem(at, EDGE) + side * (strip - EDGE)
    spread = jnp.where(iota((strip, lanes), 0) == source, 1.0, 0.0)
    copies = jnp.dot(depth, spread, precision=HIGHEST, preferred_element_type=jnp.float32)
    kept = jnp.where(iota((rows, lanes), 0) == at // EDGE, copies, 0.0)
    return jnp.sum(kept, axis=0, keepdims=True)


def kernel(
    n, lons,
    x_hbm, depth_hbm, where_hbm, values_hbm, precision_hbm, loc_hbm, count_hbm, out_ref,
    x_ref, depth_ref, values_ref, precision_ref, loc_ref, count_ref, tall32, flat16, main32, early, rim32, rim_pack, rims, edge_lo, edge_hi, west_hi, east_lo, depth_west, depth_east,
    wheres, fore, halo, cells, picks, picked, transform, result, back, out32, local_sem,
    rim_send, rim_recv, side_send, side_recv, where_send, where_recv, cell_send, cell_recv,
    pick_send, pick_recv, back_send, back_recv,
):
    me = lax.axis_index("mem")
    here = lax.axis_index("lon")
    east = lax.rem(here + 1, lons)
    west = lax.rem(here + lons - 1, lons)
    group, _, _, rows, strip = x_ref.shape
    members = n * group
    slots = where_hbm.shape[-1]
    wide = strip + 2 * MARGIN_WIDTH
    band_rows = BAND + 2 * MARGIN_WIDTH
    area = band_rows * wide
    cell = BAND * strip
    lanes = rows * EDGE
    stack = 3 * rows
    masks = list(range(n - 1, 0, -1))
    peers = {mask: xor(me, mask) for mask in masks}
    local_copies = [
        pltpu.make_async_copy(src, dst, local_sem.at[i])
        for i, (src, dst) in enumerate([
            (x_hbm, x_ref), (depth_hbm, depth_ref), (where_hbm, wheres.at[me]), (values_hbm, values_ref),
            (precision_hbm, precision_ref), (loc_hbm, loc_ref), (count_hbm, count_ref),
        ])
    ]

    barrier = pltpu.get_barrier_semaphore()
    for mask in masks:
        pl.semaphore_signal(barrier, inc=1, device_id={"mem": peers[mask]}, device_id_type=MESH)
    pl.semaphore_signal(barrier, inc=1, device_id={"lon": east}, device_id_type=MESH)
    pl.semaphore_signal(barrier, inc=1, device_id={"lon": west}, device_id_type=MESH)

    for copy in local_copies:
        copy.start()

    per = min(rows, 128 // EDGE)
    at = iota((1, 2 * per * EDGE), 1)
    inner = lax.rem(at, per * EDGE)
    source = (inner // EDGE) * strip + lax.rem(inner, EDGE) + (at // (per * EDGE)) * (strip - EDGE)
    choose = jnp.where(iota((per * strip, 2 * per * EDGE), 0) == source, 1.0, 0.0).astype(jnp.bfloat16)

    local_copies[0].wait()
    tall32[...] = x_ref[...].reshape(group * stack, strip).astype(jnp.float32)
    for c in range(3):
        for r in range(rows):
            row = tall32[pl.ds(c * rows + r, group, stride=stack), :]
            flat16[pl.ds(c * group, group), pl.ds(r * strip, strip)] = row.astype(jnp.bfloat16)

    for t in range(rows // per):
        part = jnp.dot(
            flat16[:, pl.ds(t * per * strip, per * strip)], choose, preferred_element_type=jnp.float32
        ).astype(jnp.bfloat16)
        edge_lo[:, pl.ds(t * per * EDGE, per * EDGE)] = part[:, : per * EDGE]
        edge_hi[:, pl.ds(t * per * EDGE, per * EDGE)] = part[:, per * EDGE :]

    pl.semaphore_wait(barrier, n + 1)

    def to_lon(src, dst, i, peer):
        return pltpu.make_async_remote_copy(
            src_ref=src, dst_ref=dst, send_sem=side_send.at[i], recv_sem=side_recv.at[i],
            device_id={"lon": peer}, device_id_type=MESH,
        )

    def to_mem(src, dst, ss, rs, mask):
        return pltpu.make_async_remote_copy(
            src_ref=src, dst_ref=dst, send_sem=ss, recv_sem=rs,
            device_id={"mem": peers[mask]}, device_id_type=MESH,
        )

    side_copies = [
        to_lon(edge_hi, west_hi, 0, east),
        to_lon(edge_lo, east_lo, 1, west),
        to_lon(depth_hbm, depth_west, 2, east),
        to_lon(depth_hbm, depth_east, 3, west),
    ]
    where_copies = [
        to_mem(where_hbm, wheres.at[me], where_send.at[mask], where_recv.at[mask], mask) for mask in masks
    ]
    for copy in side_copies + where_copies:
        copy.start()

    local_copies[1].wait()

    @pl.loop(0, group // CHUNK)
    def _(i):
        base = i * (CHUNK * stack)
        state = [
            [tall32[pl.ds(base + c * rows + r, CHUNK, stride=stack), :] for r in range(rows)] for c in range(3)
        ]
        depth = [depth_ref[pl.ds(r, 1), :] for r in range(rows)]
        some = pl.ds(pl.multiple_of(i * CHUNK, CHUNK), CHUNK)
        for c, field in enumerate(forecast_rows(*state, depth)):
            for r in range(rows):
                main32[c * rows + r, some, :] = field[r]
                if c == 0:
                    early[r // BAND, some, pl.ds((r % BAND) * strip, strip)] = field[r].astype(jnp.bfloat16)

    def cell_copy(src, c, mask):
        return to_mem(src, cells.at[c, me], cell_send.at[c, mask], cell_recv.at[c, mask], mask)

    cell_copies = [[cell_copy(early.at[peers[mask]], 0, mask) for mask in masks]]
    cell_copies += [[cell_copy(fore.at[peers[mask], c], c, mask) for mask in masks] for c in range(1, 3)]
    for copy in cell_copies[0]:
        copy.start()

    own_lo = pack_depth(depth_ref[...], 0, strip)
    own_hi = pack_depth(depth_ref[...], 1, strip)
    for copy in side_copies:
        copy.wait_recv()
    far_hi = pack_depth(depth_west[...], 1, strip)
    far_lo = pack_depth(depth_east[...], 0, strip)

    @pl.loop(0, group // CHUNK)
    def _(i):
        begin = pl.multiple_of(i * CHUNK, CHUNK)
        some = pl.ds(begin, CHUNK)

        def edge(ref):
            return [
                ref[pl.ds(pl.multiple_of(c * group + begin, CHUNK), CHUNK), :].astype(jnp.float32) for c in range(3)
            ]

        w_left, w_right = forecast_edge(edge(west_hi), edge(edge_lo), far_hi, own_lo, rows)
        e_left, e_right = forecast_edge(edge(edge_hi), edge(east_lo), own_hi, far_lo, rows)
        place = lax.rem(iota((1, lanes), 1), EDGE)
        column = iota((1, strip), 1)
        for c in range(3):
            outer = jnp.where(place >= MARGIN_WIDTH, w_left[c], e_right[c])
            halo[pl.ds(pl.multiple_of(c * group + begin, CHUNK), CHUNK), :] = outer.astype(jnp.bfloat16)
            rim = jnp.where(place < MARGIN_WIDTH, w_right[c], e_left[c])
            if c == 0:
                rim32[some, :] = rim
            for t in range(rows // per):
                tile = rim[:, t * per * EDGE : (t + 1) * per * EDGE]
                turned = [tile] + [pltpu.roll(tile, (per - q) * EDGE, 1) for q in range(1, per)]
                for q in range(per):
                    r = t * per + q
                    value = main32[c * rows + r, some, :]
                    value = jnp.where(column < MARGIN_WIDTH, turned[q], value)
                    value = jnp.where(column >= strip - MARGIN_WIDTH, turned[(q + 1) % per], value)
                    fore[r // BAND, c, some, pl.ds((r % BAND) * strip, strip)] = value.astype(jnp.bfloat16)

    segment = BAND * EDGE
    tile = per * EDGE
    at = iota((1, tile), 1)
    for band in range(n):
        total = jnp.zeros((CHUNK, tile), jnp.float32)
        begin = band * segment
        for q in range(group // CHUNK):
            piece = rim32[q * CHUNK : (q + 1) * CHUNK, begin // tile * tile : (begin // tile + 1) * tile]
            by = (q * segment - begin) % tile
            piece = pltpu.roll(piece, by, 1) if by else piece
            total = jnp.where(at // segment == q, piece, total)
        rim_pack[band] = total.astype(jnp.bfloat16)
    rim_copies = [
        to_mem(rim_pack.at[peers[mask]], rims.at[me], rim_send.at[mask], rim_recv.at[mask], mask) for mask in masks
    ]
    for copy in rim_copies:
        copy.start()

    for copy in where_copies:
        copy.wait_recv()
    local_copies[2].wait()
    pick_copies = []
    for mask in masks + [0]:
        band = peers[mask] if mask else me
        index = wheres[band]
        component = jnp.where(index >= area, 1, 0) + jnp.where(index >= 2 * area, 1, 0)
        rest = index - component * area
        row = jnp.zeros_like(rest)
        for q in range(1, band_rows):
            row = row + jnp.where(rest >= q * wide, 1, 0)
        column = rest - row * wide - MARGIN_WIDTH
        block = jnp.where(row >= BAND, 1, 0) + jnp.where(row >= 2 * BAND, 1, 0)
        inside = jnp.logical_and(column >= 0, column < strip)
        target = jnp.where(inside, (row - block * BAND) * strip + column, -1)
        place = jnp.where(column < 0, column + EDGE, column - strip)
        rim_target = jnp.where(inside, -1, (band * BAND - MARGIN_WIDTH + row) * EDGE + place)
        hot = jnp.where(iota((cell, slots), 0) == target, 1.0, 0.0).astype(jnp.bfloat16)
        rim_hot = jnp.where(iota((lanes, slots), 0) == rim_target, 1.0, 0.0).astype(jnp.bfloat16)
        parts = [(c, e) for c in range(3) for e in range(3)]
        table = jnp.concatenate([fore[lax.rem(band + e + n - 1, n), c] for c, e in parts], axis=0)
        found = jnp.dot(table, hot, preferred_element_type=jnp.float32)
        rim_found = jnp.dot(halo[...], rim_hot, preferred_element_type=jnp.float32)
        total = jnp.zeros((group, slots), jnp.float32)
        for q, (c, e) in enumerate(parts):
            exists = jnp.logical_and(band + e - 1 >= 0, band + e - 1 < n)
            wanted = jnp.where(exists, 3 * c + e, -1)
            total = jnp.where(3 * component + block == wanted, found[q * group : (q + 1) * group], total)
        for c in range(3):
            rim_part = rim_found[c * group : (c + 1) * group]
            total = total + jnp.where(component == c, rim_part, 0.0)
        if mask:
            picks[mask] = total.astype(jnp.bfloat16)
            copy = to_mem(picks.at[mask], picked.at[me], pick_send.at[mask], pick_recv.at[mask], mask)
            copy.start()
            pick_copies.append(copy)
        else:
            picked[me] = total.astype(jnp.bfloat16)

    for c in range(1, 3):
        for copy in cell_copies[c]:
            copy.start()
    for c in range(3):
        cells[c, me] = fore[me, c]

    column = iota((1, strip), 1)
    for copy, rim_copy, mask in zip(cell_copies[0], rim_copies, masks):
        copy.wait_recv()
        rim_copy.wait_recv()
        piece = rims[peers[mask]].astype(jnp.float32)
        for q in range(group // CHUNK):
            shifts = [(-(q * segment + b * EDGE)) % tile for b in range(BAND + 1)]
            turned = [pltpu.roll(piece, by, 1) if by else piece for by in shifts]
            for b in range(BAND):
                some = (0, peers[mask], pl.ds(q * CHUNK, CHUNK), pl.ds(b * strip, strip))
                value = cells[some].astype(jnp.float32)
                value = jnp.where(column < MARGIN_WIDTH, turned[b], value)
                value = jnp.where(column >= strip - MARGIN_WIDTH, turned[b + 1], value)
                cells[some] = value.astype(jnp.bfloat16)

    for copy in local_copies[3:]:
        copy.wait()
    live = jnp.where(iota((1, slots), 1) < count_ref[...], 1.0, 0.0)
    taper = 1.0 - loc_ref[...].astype(jnp.float32) / 16.0
    weight = precision_ref[...] * (taper * taper) * live

    for copy in pick_copies:
        copy.wait_recv()
    obs = picked[...].astype(jnp.float32).reshape(members, slots)
    obs_mean = jnp.mean(obs, axis=0, keepdims=True)
    spread = obs - obs_mean
    weighted = spread * weight
    innovation = values_ref[...] - obs_mean

    def mm(a, b):
        return jnp.dot(a, b, precision=HIGHEST, preferred_element_type=jnp.float32)

    gram = lax.dot_general(
        weighted, spread, (((1,), (1,)), ((), ())),
        precision=HIGHEST, preferred_element_type=jnp.float32,
    )
    drive = jnp.sum(weighted * innovation, axis=1, keepdims=True)
    prior = (members - 1) / inflation
    trace = jnp.sum(jnp.sum(weighted * spread, axis=1, keepdims=True), axis=0, keepdims=True)
    trace_bound = prior + trace
    identity = jnp.where(iota((members, members), 0) == iota((members, members), 1), 1.0, 0.0)
    root_iter = (gram + prior * identity) / trace_bound
    correction = 1.5 * identity - 0.5 * root_iter
    root_iter = mm(root_iter, correction)
    inv_root = correction
    for sweep in range(1, NS_ITERS):
        correction = 1.5 * identity - 0.5 * mm(inv_root, root_iter)
        if sweep < NS_ITERS - 1:
            root_iter = mm(root_iter, correction)
        inv_root = mm(correction, inv_root)
    shrink = inv_root * lax.rsqrt(trace_bound)
    inner = jnp.sum(shrink * drive, axis=0, keepdims=True)
    mean_weight = jnp.sum(shrink * inner, axis=1, keepdims=True)
    weights = math.sqrt(members - 1) * shrink + mean_weight
    weights = weights + (1.0 - jnp.sum(weights, axis=0, keepdims=True)) / members
    weights_t = weights.T
    high = weights_t.astype(jnp.bfloat16)
    transform[0] = high
    transform[1] = (weights_t - high.astype(jnp.float32)).astype(jnp.bfloat16)

    back_copies = []
    for c in range(3):
        if c > 0:
            for copy in cell_copies[c]:
                copy.wait_recv()
        all_cells = cells[c].reshape(members, cell)
        total = jnp.dot(transform[0], all_cells, preferred_element_type=jnp.float32)
        total += jnp.dot(transform[1], all_cells, preferred_element_type=jnp.float32)
        result[c] = total.astype(jnp.bfloat16).reshape(n, group, cell)
        row_copies = [
            to_mem(result.at[c, peers[mask]], back.at[c, me], back_send.at[c, mask], back_recv.at[c, mask], mask)
            for mask in masks
        ]
        for copy in row_copies:
            copy.start()
        back_copies.append(row_copies)
        back[c, me] = result[c, me]

    def place_rows(c, band):
        block = back[c, band].astype(jnp.float32)
        for q in range(BAND):
            out32[c, pl.ds(band * BAND + q, group, stride=rows), :] = block[:, q * strip : (q + 1) * strip]

    for c in range(3):
        place_rows(c, me)
        for copy, mask in zip(back_copies[c], masks):
            copy.wait_recv()
            place_rows(c, peers[mask])
        out_ref[:, c, 0] = out32[c].reshape(group, rows, strip).astype(jnp.bfloat16)

    for copy in side_copies + where_copies + pick_copies + rim_copies:
        copy.wait_send()
    for c in range(3):
        for copy in cell_copies[c] + back_copies[c]:
            copy.wait_send()


def deliver(in_ref, out_ref, sem):
    copy = pltpu.make_async_copy(in_ref, out_ref, sem)
    copy.start()
    copy.wait()


def on_device(
    sample_collection, layer_depth, obs_where, observed_values, obs_precision, loc_index, obs_count
):
    n, lons = lax.axis_size("mem"), lax.axis_size("lon")
    group, _, _, rows, strip = sample_collection.shape
    slots = obs_where.shape[-1]
    members, lanes, cell = n * group, rows * EDGE, BAND * strip
    vmem = pl.BlockSpec(memory_space=pltpu.VMEM)
    dma = pltpu.SemaphoreType.DMA
    f32, bf16 = jnp.float32, jnp.bfloat16
    scratch = [
        pltpu.VMEM(sample_collection.shape, bf16),
        pltpu.VMEM((rows, strip), f32),
        pltpu.VMEM((1, slots), f32),
        pltpu.VMEM((1, slots), f32),
        pltpu.VMEM((1, slots), jnp.int32),
        pltpu.VMEM((1, 1), jnp.int32),
        pltpu.VMEM((group * 3 * rows, strip), f32),
        pltpu.VMEM((3 * group, rows * strip), bf16),
        pltpu.VMEM((3 * rows, group, strip), f32),
        pltpu.VMEM((n, group, cell), bf16),
        pltpu.VMEM((group, lanes), f32),
        pltpu.VMEM((n, CHUNK, min(lanes, 128)), bf16),
        pltpu.VMEM((n, CHUNK, min(lanes, 128)), bf16),
    ]
    scratch += [pltpu.VMEM((3 * group, lanes), bf16)] * 4
    scratch += [pltpu.VMEM((rows, strip), f32)] * 2
    scratch += [
        pltpu.VMEM((n, 1, slots), jnp.int32),
        pltpu.VMEM((n, 3, group, cell), bf16),
        pltpu.VMEM((3 * group, lanes), bf16),
        pltpu.VMEM((3, n, group, cell), bf16),
        pltpu.VMEM((n, group, slots), bf16),
        pltpu.VMEM((n, group, slots), bf16),
        pltpu.VMEM((2, members, members), bf16),
        pltpu.VMEM((3, n, group, cell), bf16),
        pltpu.VMEM((3, n, group, cell), bf16),
        pltpu.VMEM((3, group * rows, strip), f32),
    ]
    scratch += [dma((7,))]
    scratch += [dma((n,))] * 2 + [dma((4,))] * 2 + [dma((n,))] * 2 + [dma((3, n))] * 2 + [dma((n,))] * 2 + [dma((3, n))] * 2
    out = pl.pallas_call(
        functools.partial(kernel, n, lons),
        out_shape=pltpu.VMEM(sample_collection.shape, bf16),
        in_specs=[pl.BlockSpec(memory_space=pltpu.HBM)] * 7,
        out_specs=vmem,
        scratch_shapes=scratch,
        compiler_params=pltpu.CompilerParams(
            collective_id=0, has_side_effects=True, vmem_limit_bytes=60 * 1024 * 1024
        ),
    )(
        sample_collection, layer_depth[0], obs_where[0], observed_values[0],
        obs_precision[0], loc_index[0], obs_count,
    )
    return pl.pallas_call(
        deliver,
        out_shape=jax.ShapeDtypeStruct(sample_collection.shape, bf16),
        in_specs=[vmem],
        out_specs=pl.BlockSpec(memory_space=pl.ANY),
        scratch_shapes=[dma(())],
        compiler_params=pltpu.CompilerParams(vmem_limit_bytes=4 * 1024 * 1024),
    )(out)


def solution(mesh):
    in_specs = (
        P("mem", None, None, None, "lon"),
        P(None, None, "lon"),
        P("mem", "lon", None),
        P("mem", "lon", None),
        P("mem", "lon", None),
        P("mem", "lon", None),
        P("mem", "lon"),
    )
    out_specs = P("mem", None, None, None, "lon")
    return jax.shard_map(
        on_device, mesh=mesh, in_specs=in_specs, out_specs=out_specs, check_vma=False
    )
```

```python
import functools
import math

import jax
import jax.numpy as jnp
from jax import lax
from jax.experimental import pallas as pl
from jax.experimental.pallas import tpu as pltpu
from jax.sharding import PartitionSpec as P

STEPS = 2
MARGIN_WIDTH = 4
BAND = 4
NS_ITERS = 5
EDGE = 8
CHUNK = 16
MESH = pl.DeviceIdType.MESH
HIGHEST = lax.Precision.HIGHEST

time_step = 0.8
inflation = 1.1
half_step = 0.5 * time_step


def iota(shape, axis):
    return lax.broadcasted_iota(jnp.int32, shape, axis)


def xor(me, mask):
    out = me
    bit = 1
    while bit <= mask:
        if mask & bit:
            out = out + bit - 2 * bit * lax.rem(me // bit, 2)
        bit *= 2
    return out


def spin(row, count_rows):
    return 0.4 * (row / (count_rows - 1) - 0.5)


def forecast_rows(h, u, v, depth):
    rows = len(h)
    wide = h[0].shape[-1]
    for _ in range(STEPS):
        flux_east = [depth[r] * u[r] for r in range(rows)]
        flux_north = [depth[r] * v[r] for r in range(rows)]
        h_new = []
        for r in range(rows):
            change = pltpu.roll(flux_east[r], wide - 1, 1) - pltpu.roll(flux_east[r], 1, 1)
            if r + 1 < rows:
                change = change + flux_north[r + 1]
            if r > 0:
                change = change - flux_north[r - 1]
            h_new.append(h[r] - half_step * change)
        u_new, v_new = [], []
        for r in range(rows):
            turn = time_step * spin(r, rows)
            slope = pltpu.roll(h_new[r], wide - 1, 1) - pltpu.roll(h_new[r], 1, 1)
            u_new.append(u[r] - half_step * slope + turn * v[r])
            new = v[r] - turn * u[r]
            if r + 1 < rows:
                new = new - half_step * h_new[r + 1]
            if r > 0:
                new = new + half_step * h_new[r - 1]
            v_new.append(new)
        h, u, v = h_new, u_new, v_new
    return h, u, v


def forecast_edge(left, right, depth_left, depth_right, rows):
    lanes = rows * EDGE
    at = iota((1, lanes), 1)
    place = lax.rem(at, EDGE)
    row = at // EDGE
    turn = time_step * 0.4 * (row.astype(jnp.float32) / (rows - 1) - 0.5)

    def shift(x, by):
        return pltpu.roll(x, by % lanes, 1)

    def lon(x_left, x_right):
        d_left = jnp.where(place == EDGE - 1, shift(x_right, EDGE - 1), shift(x_left, -1)) - shift(x_left, 1)
        d_right = shift(x_right, -1) - jnp.where(place == 0, shift(x_left, 1 - EDGE), shift(x_right, 1))
        return d_left, d_right

    def lat(x):
        north = jnp.where(row == rows - 1, 0.0, shift(x, -EDGE))
        south = jnp.where(row == 0, 0.0, shift(x, EDGE))
        return north - south

    for _ in range(STEPS):
        (h_l, u_l, v_l), (h_r, u_r, v_r) = left, right
        d_l, d_r = lon(depth_left * u_l, depth_right * u_r)
        n_l = h_l - half_step * (d_l + lat(depth_left * v_l))
        n_r = h_r - half_step * (d_r + lat(depth_right * v_r))
        s_l, s_r = lon(n_l, n_r)
        left = (n_l, u_l - half_step * s_l + turn * v_l, v_l - half_step * lat(n_l) - turn * u_l)
        right = (n_r, u_r - half_step * s_r + turn * v_r, v_r - half_step * lat(n_r) - turn * u_r)
    return left, right


def pack_depth(depth, side, strip):
    rows = depth.shape[0]
    lanes = rows * EDGE
    at = iota((1, lanes), 1)
    source = lax.rem(at, EDGE) + side * (strip - EDGE)
    spread = jnp.where(iota((strip, lanes), 0) == source, 1.0, 0.0)
    copies = jnp.dot(depth, spread, precision=HIGHEST, preferred_element_type=jnp.float32)
    kept = jnp.where(iota((rows, lanes), 0) == at // EDGE, copies, 0.0)
    return jnp.sum(kept, axis=0, keepdims=True)


def kernel(
    n, lons,
    x_hbm, depth_hbm, where_hbm, values_hbm, precision_hbm, loc_hbm, count_hbm, out_ref,
    x_ref, depth_ref, values_ref, precision_ref, loc_ref, count_ref, tall32, flat16, main32, early, rim32, rim_pack, rims, edge_lo, edge_hi, west_hi, east_lo, depth_west, depth_east,
    wheres, fore, halo, cells, picks, picked, transform, result, back, out32, local_sem,
    early_send, early_recv, rim_send, rim_recv, side_send, side_recv, where_send, where_recv, cell_send, cell_recv,
    pick_send, pick_recv, back_send, back_recv,
):
    me = lax.axis_index("mem")
    here = lax.axis_index("lon")
    east = lax.rem(here + 1, lons)
    west = lax.rem(here + lons - 1, lons)
    group, _, _, rows, strip = x_ref.shape
    members = n * group
    slots = where_hbm.shape[-1]
    wide = strip + 2 * MARGIN_WIDTH
    band_rows = BAND + 2 * MARGIN_WIDTH
    area = band_rows * wide
    cell = BAND * strip
    lanes = rows * EDGE
    stack = 3 * rows
    masks = sorted(range(1, n), key=lambda mask: (mask.bit_count(), -mask))
    peers = {mask: xor(me, mask) for mask in masks}
    local_copies = [
        pltpu.make_async_copy(src, dst, local_sem.at[i])
        for i, (src, dst) in enumerate([
            (x_hbm, x_ref), (depth_hbm, depth_ref), (where_hbm, wheres.at[me]), (values_hbm, values_ref),
            (precision_hbm, precision_ref), (loc_hbm, loc_ref), (count_hbm, count_ref),
        ])
    ]

    barrier = pltpu.get_barrier_semaphore()
    for mask in masks:
        pl.semaphore_signal(barrier, inc=1, device_id={"mem": peers[mask]}, device_id_type=MESH)
    pl.semaphore_signal(barrier, inc=1, device_id={"lon": east}, device_id_type=MESH)
    pl.semaphore_signal(barrier, inc=1, device_id={"lon": west}, device_id_type=MESH)

    for copy in local_copies:
        copy.start()

    per = min(rows, 128 // EDGE)
    at = iota((1, 2 * per * EDGE), 1)
    inner = lax.rem(at, per * EDGE)
    source = (inner // EDGE) * strip + lax.rem(inner, EDGE) + (at // (per * EDGE)) * (strip - EDGE)
    choose = jnp.where(iota((per * strip, 2 * per * EDGE), 0) == source, 1.0, 0.0).astype(jnp.bfloat16)

    local_copies[0].wait()
    tall32[...] = x_ref[...].reshape(group * stack, strip).astype(jnp.float32)
    for c in range(3):
        for r in range(rows):
            row = tall32[pl.ds(c * rows + r, group, stride=stack), :]
            flat16[pl.ds(c * group, group), pl.ds(r * strip, strip)] = row.astype(jnp.bfloat16)

    for t in range(rows // per):
        part = jnp.dot(
            flat16[:, pl.ds(t * per * strip, per * strip)], choose, preferred_element_type=jnp.float32
        ).astype(jnp.bfloat16)
        edge_lo[:, pl.ds(t * per * EDGE, per * EDGE)] = part[:, : per * EDGE]
        edge_hi[:, pl.ds(t * per * EDGE, per * EDGE)] = part[:, per * EDGE :]

    pl.semaphore_wait(barrier, n + 1)

    def to_lon(src, dst, i, peer):
        return pltpu.make_async_remote_copy(
            src_ref=src, dst_ref=dst, send_sem=side_send.at[i], recv_sem=side_recv.at[i],
            device_id={"lon": peer}, device_id_type=MESH,
        )

    def to_mem(src, dst, ss, rs, mask):
        return pltpu.make_async_remote_copy(
            src_ref=src, dst_ref=dst, send_sem=ss, recv_sem=rs,
            device_id={"mem": peers[mask]}, device_id_type=MESH,
        )

    side_copies = [
        to_lon(edge_hi, west_hi, 0, east),
        to_lon(edge_lo, east_lo, 1, west),
        to_lon(depth_hbm, depth_west, 2, east),
        to_lon(depth_hbm, depth_east, 3, west),
    ]
    where_copies = [
        to_mem(where_hbm, wheres.at[me], where_send.at[mask], where_recv.at[mask], mask) for mask in masks
    ]
    for copy in side_copies + where_copies:
        copy.start()

    local_copies[1].wait()

    def early_copy(i, mask):
        some = pl.ds(pl.multiple_of(i * CHUNK, CHUNK), CHUNK)
        return to_mem(
            early.at[peers[mask], some], cells.at[0, me, some], early_send.at[i, mask], early_recv.at[i, mask], mask
        )

    @pl.loop(0, group // CHUNK)
    def _(i):
        base = i * (CHUNK * stack)
        state = [
            [tall32[pl.ds(base + c * rows + r, CHUNK, stride=stack), :] for r in range(rows)] for c in range(3)
        ]
        depth = [depth_ref[pl.ds(r, 1), :] for r in range(rows)]
        some = pl.ds(pl.multiple_of(i * CHUNK, CHUNK), CHUNK)
        for c, field in enumerate(forecast_rows(*state, depth)):
            for r in range(rows):
                main32[c * rows + r, some, :] = field[r]
                if c == 0:
                    early[r // BAND, some, pl.ds((r % BAND) * strip, strip)] = field[r].astype(jnp.bfloat16)
        for mask in masks:
            early_copy(i, mask).start()

    own_lo = pack_depth(depth_ref[...], 0, strip)
    own_hi = pack_depth(depth_ref[...], 1, strip)
    for copy in side_copies:
        copy.wait_recv()
    far_hi = pack_depth(depth_west[...], 1, strip)
    far_lo = pack_depth(depth_east[...], 0, strip)

    @pl.loop(0, group // CHUNK)
    def _(i):
        begin = pl.multiple_of(i * CHUNK, CHUNK)
        some = pl.ds(begin, CHUNK)

        def edge(ref):
            return [
                ref[pl.ds(pl.multiple_of(c * group + begin, CHUNK), CHUNK), :].astype(jnp.float32) for c in range(3)
            ]

        w_left, w_right = forecast_edge(edge(west_hi), edge(edge_lo), far_hi, own_lo, rows)
        e_left, e_right = forecast_edge(edge(edge_hi), edge(east_lo), own_hi, far_lo, rows)
        place = lax.rem(iota((1, lanes), 1), EDGE)
        column = iota((1, strip), 1)
        for c in range(3):
            outer = jnp.where(place >= MARGIN_WIDTH, w_left[c], e_right[c])
            halo[pl.ds(pl.multiple_of(c * group + begin, CHUNK), CHUNK), :] = outer.astype(jnp.bfloat16)
            rim = jnp.where(place < MARGIN_WIDTH, w_right[c], e_left[c])
            if c == 0:
                rim32[some, :] = rim
            for t in range(rows // per):
                tile = rim[:, t * per * EDGE : (t + 1) * per * EDGE]
                turned = [tile] + [pltpu.roll(tile, (per - q) * EDGE, 1) for q in range(1, per)]
                for q in range(per):
                    r = t * per + q
                    value = main32[c * rows + r, some, :]
                    value = jnp.where(column < MARGIN_WIDTH, turned[q], value)
                    value = jnp.where(column >= strip - MARGIN_WIDTH, turned[(q + 1) % per], value)
                    fore[r // BAND, c, some, pl.ds((r % BAND) * strip, strip)] = value.astype(jnp.bfloat16)

    cell_copies = [
        [
            to_mem(fore.at[peers[mask], c], cells.at[c, me], cell_send.at[c, mask], cell_recv.at[c, mask], mask)
            for mask in masks
        ]
        for c in range(1, 3)
    ]
    early_copies = {mask: [early_copy(i, mask) for i in range(group // CHUNK)] for mask in masks}

    segment = BAND * EDGE
    tile = per * EDGE
    at = iota((1, tile), 1)
    for band in range(n):
        total = jnp.zeros((CHUNK, tile), jnp.float32)
        begin = band * segment
        for q in range(group // CHUNK):
            piece = rim32[q * CHUNK : (q + 1) * CHUNK, begin // tile * tile : (begin // tile + 1) * tile]
            by = (q * segment - begin) % tile
            piece = pltpu.roll(piece, by, 1) if by else piece
            total = jnp.where(at // segment == q, piece, total)
        rim_pack[band] = total.astype(jnp.bfloat16)
    rim_copies = [
        to_mem(rim_pack.at[peers[mask]], rims.at[me], rim_send.at[mask], rim_recv.at[mask], mask) for mask in masks
    ]
    for copy in rim_copies:
        copy.start()

    for copy in cell_copies[0][:1]:
        copy.start()
    for copy in where_copies:
        copy.wait_recv()
    local_copies[2].wait()
    pick_copies = []
    for mask in masks + [0]:
        band = peers[mask] if mask else me
        index = wheres[band]
        component = jnp.where(index >= area, 1, 0) + jnp.where(index >= 2 * area, 1, 0)
        rest = index - component * area
        row = jnp.zeros_like(rest)
        for q in range(1, band_rows):
            row = row + jnp.where(rest >= q * wide, 1, 0)
        column = rest - row * wide - MARGIN_WIDTH
        block = jnp.where(row >= BAND, 1, 0) + jnp.where(row >= 2 * BAND, 1, 0)
        inside = jnp.logical_and(column >= 0, column < strip)
        target = jnp.where(inside, (row - block * BAND) * strip + column, -1)
        place = jnp.where(column < 0, column + EDGE, column - strip)
        rim_target = jnp.where(inside, -1, (band * BAND - MARGIN_WIDTH + row) * EDGE + place)
        hot = jnp.where(iota((cell, slots), 0) == target, 1.0, 0.0).astype(jnp.bfloat16)
        rim_hot = jnp.where(iota((lanes, slots), 0) == rim_target, 1.0, 0.0).astype(jnp.bfloat16)
        parts = [(c, e) for c in range(3) for e in range(3)]
        table = jnp.concatenate([fore[lax.rem(band + e + n - 1, n), c] for c, e in parts], axis=0)
        found = jnp.dot(table, hot, preferred_element_type=jnp.float32)
        rim_found = jnp.dot(halo[...], rim_hot, preferred_element_type=jnp.float32)
        total = jnp.zeros((group, slots), jnp.float32)
        for q, (c, e) in enumerate(parts):
            exists = jnp.logical_and(band + e - 1 >= 0, band + e - 1 < n)
            wanted = jnp.where(exists, 3 * c + e, -1)
            total = jnp.where(3 * component + block == wanted, found[q * group : (q + 1) * group], total)
        for c in range(3):
            rim_part = rim_found[c * group : (c + 1) * group]
            total = total + jnp.where(component == c, rim_part, 0.0)
        if mask:
            picks[mask] = total.astype(jnp.bfloat16)
            copy = to_mem(picks.at[mask], picked.at[me], pick_send.at[mask], pick_recv.at[mask], mask)
            copy.start()
            pick_copies.append(copy)
        else:
            picked[me] = total.astype(jnp.bfloat16)

    for copy in cell_copies[0][1:] + cell_copies[1]:
        copy.start()
    for c in range(3):
        cells[c, me] = fore[me, c]

    column = iota((1, strip), 1)
    for rim_copy, mask in zip(rim_copies, masks):
        for copy in early_copies[mask]:
            copy.wait_recv()
        rim_copy.wait_recv()
        piece = rims[peers[mask]].astype(jnp.float32)
        for q in range(group // CHUNK):
            shifts = [(-(q * segment + b * EDGE)) % tile for b in range(BAND + 1)]
            turned = [pltpu.roll(piece, by, 1) if by else piece for by in shifts]
            for b in range(BAND):
                some = (0, peers[mask], pl.ds(q * CHUNK, CHUNK), pl.ds(b * strip, strip))
                value = cells[some].astype(jnp.float32)
                value = jnp.where(column < MARGIN_WIDTH, turned[b], value)
                value = jnp.where(column >= strip - MARGIN_WIDTH, turned[b + 1], value)
                cells[some] = value.astype(jnp.bfloat16)

    for copy in local_copies[3:]:
        copy.wait()
    live = jnp.where(iota((1, slots), 1) < count_ref[...], 1.0, 0.0)
    taper = 1.0 - loc_ref[...].astype(jnp.float32) / 16.0
    weight = precision_ref[...] * (taper * taper) * live

    for copy in pick_copies:
        copy.wait_recv()
    obs = picked[...].astype(jnp.float32).reshape(members, slots)
    obs_mean = jnp.mean(obs, axis=0, keepdims=True)
    spread = obs - obs_mean
    weighted = spread * weight
    innovation = values_ref[...] - obs_mean

    def mm(a, b):
        return jnp.dot(a, b, precision=HIGHEST, preferred_element_type=jnp.float32)

    gram = lax.dot_general(
        weighted, spread, (((1,), (1,)), ((), ())),
        precision=HIGHEST, preferred_element_type=jnp.float32,
    )
    drive = jnp.sum(weighted * innovation, axis=1, keepdims=True)
    prior = (members - 1) / inflation
    trace = jnp.sum(jnp.sum(weighted * spread, axis=1, keepdims=True), axis=0, keepdims=True)
    trace_bound = prior + trace
    identity = jnp.where(iota((members, members), 0) == iota((members, members), 1), 1.0, 0.0)
    root_iter = (gram + prior * identity) / trace_bound
    correction = 1.5 * identity - 0.5 * root_iter
    root_iter = mm(root_iter, correction)
    inv_root = correction
    for sweep in range(1, NS_ITERS):
        correction = 1.5 * identity - 0.5 * mm(inv_root, root_iter)
        if sweep < NS_ITERS - 1:
            root_iter = mm(root_iter, correction)
        inv_root = mm(correction, inv_root)
    shrink = inv_root * lax.rsqrt(trace_bound)
    inner = jnp.sum(shrink * drive, axis=0, keepdims=True)
    mean_weight = jnp.sum(shrink * inner, axis=1, keepdims=True)
    weights = math.sqrt(members - 1) * shrink + mean_weight
    weights = weights + (1.0 - jnp.sum(weights, axis=0, keepdims=True)) / members
    weights_t = weights.T
    high = weights_t.astype(jnp.bfloat16)
    transform[0] = high
    transform[1] = (weights_t - high.astype(jnp.float32)).astype(jnp.bfloat16)

    back_copies = []
    for c in range(3):
        if c > 0:
            for copy in cell_copies[c - 1]:
                copy.wait_recv()
        all_cells = cells[c].reshape(members, cell)
        total = jnp.dot(transform[0], all_cells, preferred_element_type=jnp.float32)
        total += jnp.dot(transform[1], all_cells, preferred_element_type=jnp.float32)
        result[c] = total.astype(jnp.bfloat16).reshape(n, group, cell)
        row_copies = [
            to_mem(result.at[c, peers[mask]], back.at[c, me], back_send.at[c, mask], back_recv.at[c, mask], mask)
            for mask in masks
        ]
        for copy in row_copies:
            copy.start()
        back_copies.append(row_copies)
        back[c, me] = result[c, me]

    def place_rows(c, band):
        block = back[c, band].astype(jnp.float32)
        for q in range(BAND):
            out32[c, pl.ds(band * BAND + q, group, stride=rows), :] = block[:, q * strip : (q + 1) * strip]

    for c in range(3):
        place_rows(c, me)
        for copy, mask in zip(back_copies[c], masks):
            copy.wait_recv()
            place_rows(c, peers[mask])
        out_ref[:, c, 0] = out32[c].reshape(group, rows, strip).astype(jnp.bfloat16)

    for copy in side_copies + where_copies + pick_copies + rim_copies:
        copy.wait_send()
    for row_copies in cell_copies + back_copies + list(early_copies.values()):
        for copy in row_copies:
            copy.wait_send()


def deliver(in_ref, out_ref, sem):
    copy = pltpu.make_async_copy(in_ref, out_ref, sem)
    copy.start()
    copy.wait()


def on_device(
    sample_collection, layer_depth, obs_where, observed_values, obs_precision, loc_index, obs_count
):
    n, lons = lax.axis_size("mem"), lax.axis_size("lon")
    group, _, _, rows, strip = sample_collection.shape
    slots = obs_where.shape[-1]
    members, lanes, cell = n * group, rows * EDGE, BAND * strip
    vmem = pl.BlockSpec(memory_space=pltpu.VMEM)
    dma = pltpu.SemaphoreType.DMA
    f32, bf16 = jnp.float32, jnp.bfloat16
    scratch = [
        pltpu.VMEM(sample_collection.shape, bf16),
        pltpu.VMEM((rows, strip), f32),
        pltpu.VMEM((1, slots), f32),
        pltpu.VMEM((1, slots), f32),
        pltpu.VMEM((1, slots), jnp.int32),
        pltpu.VMEM((1, 1), jnp.int32),
        pltpu.VMEM((group * 3 * rows, strip), f32),
        pltpu.VMEM((3 * group, rows * strip), bf16),
        pltpu.VMEM((3 * rows, group, strip), f32),
        pltpu.VMEM((n, group, cell), bf16),
        pltpu.VMEM((group, lanes), f32),
        pltpu.VMEM((n, CHUNK, min(lanes, 128)), bf16),
        pltpu.VMEM((n, CHUNK, min(lanes, 128)), bf16),
    ]
    scratch += [pltpu.VMEM((3 * group, lanes), bf16)] * 4
    scratch += [pltpu.VMEM((rows, strip), f32)] * 2
    scratch += [
        pltpu.VMEM((n, 1, slots), jnp.int32),
        pltpu.VMEM((n, 3, group, cell), bf16),
        pltpu.VMEM((3 * group, lanes), bf16),
        pltpu.VMEM((3, n, group, cell), bf16),
        pltpu.VMEM((n, group, slots), bf16),
        pltpu.VMEM((n, group, slots), bf16),
        pltpu.VMEM((2, members, members), bf16),
        pltpu.VMEM((3, n, group, cell), bf16),
        pltpu.VMEM((3, n, group, cell), bf16),
        pltpu.VMEM((3, group * rows, strip), f32),
    ]
    scratch += [dma((7,))]
    scratch += [dma((group // CHUNK, n))] * 2 + [dma((n,))] * 2 + [dma((4,))] * 2 + [dma((n,))] * 2 + [dma((3, n))] * 2 + [dma((n,))] * 2 + [dma((3, n))] * 2
    out = pl.pallas_call(
        functools.partial(kernel, n, lons),
        out_shape=pltpu.VMEM(sample_collection.shape, bf16),
        in_specs=[pl.BlockSpec(memory_space=pltpu.HBM)] * 7,
        out_specs=vmem,
        scratch_shapes=scratch,
        compiler_params=pltpu.CompilerParams(
            collective_id=0, has_side_effects=True, vmem_limit_bytes=60 * 1024 * 1024
        ),
    )(
        sample_collection, layer_depth[0], obs_where[0], observed_values[0],
        obs_precision[0], loc_index[0], obs_count,
    )
    return pl.pallas_call(
        deliver,
        out_shape=jax.ShapeDtypeStruct(sample_collection.shape, bf16),
        in_specs=[vmem],
        out_specs=pl.BlockSpec(memory_space=pl.ANY),
        scratch_shapes=[dma(())],
        compiler_params=pltpu.CompilerParams(vmem_limit_bytes=4 * 1024 * 1024),
    )(out)


def solution(mesh):
    in_specs = (
        P("mem", None, None, None, "lon"),
        P(None, None, "lon"),
        P("mem", "lon", None),
        P("mem", "lon", None),
        P("mem", "lon", None),
        P("mem", "lon", None),
        P("mem", "lon"),
    )
    out_specs = P("mem", None, None, None, "lon")
    return jax.shard_map(
        on_device, mesh=mesh, in_specs=in_specs, out_specs=out_specs, check_vma=False
    )
```
